128 devices in a mesh: rep: 4 (over y), wide: 32 (over x, z, core).
Axes of the slice: x: 4, y: 4, z: 4, core: 2. Of those that a mesh axis runs over, the one named last changes fastest.
Arguments:
- hot_table: bfloat16 [65536, 128], P('wide'), may hold values from -3 to 3
- cold_table: bfloat16 [262144, 128], P(('rep', 'wide')), may hold values from -3 to 3
- bag_of: int32 [128, 6144], P(('rep', 'wide')), may hold values from 0 to 4095, never falling along the last dimension, each value on 1 to 4 neighbouring positions
- owner: int32 [786432, 1], P(('rep', 'wide')), may hold values from 0 to 159; in each aligned block of 6144 rows (0 to 6143, 6144 to 12287, ...) at most 64 rows name the same one
- row_in: int32 [786432], P(('rep', 'wide')), may hold values from 0 to 2047
- cross_down: bfloat16 [4096, 256], replicated, may hold values from -0.09375 to 0.09375
- cross_up: bfloat16 [4096, 256], replicated, may hold values from -0.375 to 0.375
- cross_bias: float32 [4096], replicated, may hold values from -3 to 3
- top_weight: bfloat16 [4096, 512], replicated, may hold values from -0.09375 to 0.09375
- d_hidden: bfloat16 [16384, 512], P(('rep', 'wide')), may hold values from -6 to 6
Outputs:
- grad_up: float32 [4096, 256], P(('rep', 'wide'))
- grad_down: float32 [4096, 256], P(('rep', 'wide'))
- grad_top: float32 [4096, 512], P(('rep', 'wide'))
- hot_grad: float32 [65536, 128], P('wide')
- cold_grad: float32 [262144, 128], P(('rep', 'wide'))
The draws below stay inside these ranges and needn't reach their ends.
Inputs may be any that keep to these rules, and one draw needn't show every extreme that they name: Destination of each lookup: below 32 the holder of hot rows at that wide index in the asking device's own rep group, else the holder of cold rows numbered owner minus 32 over rep+wide. Among the 6144 lookups of one device no destination is named more than 64 times, and in every draw some device names some destination exactly 64 times. `bag_of`: never falls along one device's lookups; each of a device's 4096 bags has 1 to 4 lookups, and some bag has 4. Bag b is sample b // 32, feature b % 32 of the device.
All inputs are finite; a program needn't handle non-finite values.
Results may differ from the reference program's by a relative error of at most 0.0064.
Values may be sent and summed in bfloat16 or wider, within the bound.
A program may use at most 128 MiB of HBM per device.

```python
import math
import jax
import jax.numpy as jnp
import numpy as np
from jax import lax

E = 128
R = 256
H = 512
MOST = 4
B_DEV = 128
ROWS_DEV = 2048
D = 4096
BAGS_DEV = 4096
LOOK_DEV = 6144
SHARDS = 128
DESTS = 160
CAP = 64
BATCH = 16384
LOOKUPS = 786432
HOT = 65536
COLD = 262144
N_WIDE = 32


def set_ends(values, key, least, top_value):
    longest = values.shape.index(max(values.shape))
    spots = []
    for shift in (0, 1):
        where = [jax.random.randint(jax.random.fold_in(key, axis), (), 0, length) for axis, length in enumerate(values.shape)]
        where[longest] = (where[longest] + shift) % values.shape[longest]
        spots.append(tuple(where))
    return values.at[spots[0]].set(least).at[spots[1]].set(top_value)


def block_scale(key, shape, cuts, low, top_value):
    level, own = 1.0, jax.random.fold_in(key, 6)
    for axis_at, shards_of in cuts:
        steps = jnp.exp(jax.random.uniform(jax.random.fold_in(own, axis_at), (shards_of,), jnp.float32, low / len(cuts), top_value / len(cuts)))
        level = level * jnp.repeat(steps, shape[axis_at] // shards_of).reshape([-1 if axis == axis_at else 1 for axis in range(len(shape))])
    return level


def profile(amount, total, limit, slope):
    portions = [(1 << 20) // math.isqrt(rank ** slope) + 1 for rank in range(2, amount + 1)]
    rest, counts = total - limit - (amount - 1), [1] * (amount - 1)
    while rest > 0:
        free = [i for i in range(amount - 1) if counts[i] < limit]
        whole, budget = sum([portions[i] for i in free]), rest
        for i in free:
            addition = min(limit - counts[i], max(1, budget * portions[i] // whole), rest)
            counts[i] = counts[i] + addition
            rest = rest - addition
    return np.array([limit] + counts)


def ragged_sizes(stream_key, count, total, most, skew):
    if count == 2:
        one = jax.random.randint(stream_key, (), max(1, total - most), min(most, total - 1) + 1)
        return jnp.stack([one, total - one])
    tallies = jnp.asarray(profile(count, total, most, skew), jnp.int32)
    pairs = (count - 1) // 2
    giver, taker = tallies[1:1 + 2 * pairs:2], tallies[2:2 + 2 * pairs:2]
    room = jnp.minimum(giver - 1, most - taker)
    shifted = jax.random.randint(jax.random.fold_in(stream_key, 1), (pairs,), 0, 1 << 20) % (room + 1)
    tallies = tallies.at[1:1 + 2 * pairs:2].set(giver - shifted).at[2:2 + 2 * pairs:2].set(taker + shifted)
    return tallies[jax.random.permutation(jax.random.fold_in(stream_key, 2), count)]


def routed_block(own_key, own, number, rows, amount, top, reach, slope):
    ranking = jax.random.permutation(own_key, amount)
    heavy_load, ordinary = shares(amount, rows * top, reach, slope, True), shares(amount, rows * top, reach, slope, False)
    places = jnp.arange(amount)

    def named(lengths, offset_by):
        used = int((lengths > 0).sum())
        fixed = max(1, used // 4)
        shifted = fixed + (places - fixed + offset_by * (used - fixed)) % max(1, amount - fixed)
        return jnp.zeros((amount,), jnp.int32).at[ranking[jnp.where(places < fixed, places, shifted)]].set(jnp.asarray(lengths, jnp.int32))

    lengths = jnp.where(number % 4 == 0, named(heavy_load, number // 4), named(ordinary, number - number // 4 - 1))
    mixed = jax.random.permutation(jax.random.fold_in(own, 3), amount)
    donor, taker = mixed[0:amount // 2 * 2:2], mixed[1:amount // 2 * 2:2]
    slack = jnp.minimum(lengths[donor] - 1, reach - lengths[taker]) // 2
    slack = jnp.where((donor == ranking[0]) | (taker == ranking[0]) | (lengths[taker] == 0), 0, jnp.maximum(slack, 0))
    shifted = jax.random.randint(jax.random.fold_in(own, 4), (amount // 2,), 0, 1 << 20) % (slack + 1)
    lengths = lengths.at[donor].add(-shifted).at[taker].add(shifted)
    labels = jnp.searchsorted(jnp.cumsum(lengths), jnp.arange(rows * top), side="right").astype(jnp.int32)
    grid = labels.reshape(top, rows).T
    grid = grid[jax.random.permutation(jax.random.fold_in(own, 1), rows)]
    offset_by = jax.random.randint(jax.random.fold_in(own, 2), (rows, 1), 0, top)
    return jnp.take_along_axis(grid, (jnp.arange(top)[None, :] + offset_by) % top, axis=1)


def shares(count, total, bound, skew, full):
    weights = [(1 << 20) // math.isqrt(grade ** skew) + 1 for grade in range(1, count + 1)]
    largest = bound if full else min(bound, max(-(-total // count), total * weights[0] // sum(weights)))
    least = 1 if total - largest >= count - 1 else 0
    given, rest = [largest] + [least] * (count - 1), total - largest - least * (count - 1)
    while rest > 0:
        free = [i for i in range(1, count) if given[i] < largest] or [i for i in range(1, count) if given[i] < bound]
        mass, budget = sum([weights[i] for i in free]), rest
        for i in free:
            extra = min(bound - given[i], max(1, budget * weights[i] // mass), rest)
            given[i] = given[i] + extra
            rest = rest - extra
    return np.array(given)


def gaussian(rng, dims, width, bound, shards=(), kind=jnp.bfloat16):
    loudness = block_scale(rng, dims, shards, -0.22, 0.18) if shards else 1.0
    entries = jax.random.normal(rng, dims, jnp.float32) * width * loudness
    return jnp.minimum(jnp.maximum(entries, -bound), bound).astype(kind)


def setup_inputs(seed: int = 0) -> dict:
    arg_keys = jax.random.split(jax.random.key(seed), 11)
    hot_table = gaussian(arg_keys[0], (HOT, E), 0.5, 3.0, ((0, 32),))
    cold_table = gaussian(arg_keys[1], (COLD, E), 0.5, 3.0, ((0, 128),))
    bag_of = jax.vmap(lambda own: jnp.searchsorted(jnp.cumsum(ragged_sizes(own, BAGS_DEV, LOOK_DEV, MOST, 2)), jnp.arange(LOOK_DEV), side="right"))(jax.random.split(arg_keys[2], SHARDS)).reshape((SHARDS, LOOK_DEV)).astype(jnp.int32)
    owner_keys = jax.random.split(jax.random.fold_in(arg_keys[3], 1), LOOKUPS // LOOK_DEV)
    owner_turns = jax.random.permutation(jax.random.fold_in(arg_keys[3], 3), LOOKUPS // LOOK_DEV)
    owner = jax.vmap(lambda own, number: routed_block(jax.random.fold_in(arg_keys[3], 2), own, number, LOOK_DEV, DESTS, 1, CAP, 2))(owner_keys, owner_turns).reshape((LOOKUPS, 1))
    row_in = set_ends(jax.random.randint(arg_keys[4], (LOOKUPS,), 0, ROWS_DEV), jax.random.fold_in(arg_keys[4], 1), 0, ROWS_DEV - 1).astype(jnp.int32)
    cross_down = gaussian(arg_keys[5], (D, R), D ** -0.5, 0.09375)
    cross_up = gaussian(arg_keys[6], (D, R), R ** -0.5, 0.375)
    cross_bias = gaussian(arg_keys[7], (D,), 0.5, 3.0, (), jnp.float32)
    top_weight = gaussian(arg_keys[8], (D, H), D ** -0.5, 0.09375)
    d_hidden = gaussian(arg_keys[9], (BATCH, H), 1.0, 6.0, ((0, 128),))
    return dict(hot_table=hot_table, cold_table=cold_table, bag_of=bag_of, owner=owner, row_in=row_in, cross_down=cross_down, cross_up=cross_up, cross_bias=cross_bias, top_weight=top_weight, d_hidden=d_hidden)


def dense_pass(base, grad_hidden, cross_down, cross_up, cross_bias, top_weight):
    low = jnp.dot(base, cross_down, preferred_element_type=jnp.float32).astype(jnp.bfloat16)
    cross = lax.dot_general(low, cross_up, (((1,), (1,)), ((), ())), preferred_element_type=jnp.float32) + cross_bias
    base_full = base.astype(jnp.float32)
    mixed = (base_full * cross + base_full).astype(jnp.bfloat16)
    preact = jnp.dot(mixed, top_weight, preferred_element_type=jnp.float32)
    sigm = jax.nn.sigmoid(preact)
    d_pre = (grad_hidden.astype(jnp.float32) * sigm * (1.0 + preact * (1.0 - sigm))).astype(jnp.bfloat16)
    d_mixed = lax.dot_general(d_pre, top_weight, (((1,), (1,)), ((), ())), preferred_element_type=jnp.float32)
    d_cross = (d_mixed * base_full).astype(jnp.bfloat16)
    d_low = jnp.dot(d_cross, cross_up, preferred_element_type=jnp.float32).astype(jnp.bfloat16)
    d_base = (d_mixed * (cross + 1.0) + lax.dot_general(d_low, cross_down, (((1,), (1,)), ((), ())), preferred_element_type=jnp.float32)).astype(jnp.bfloat16)
    contract = (((0,), (0,)), ((), ()))
    t_up = lax.dot_general(d_cross, low, contract, preferred_element_type=jnp.float32)
    t_down = lax.dot_general(base, d_low, contract, preferred_element_type=jnp.float32)
    t_top = lax.dot_general(mixed, d_pre, contract, preferred_element_type=jnp.float32)
    return (jnp.concatenate([t_up, t_down, t_top], axis=1), d_base)

def reference(hot_table, cold_table, bag_of, owner, row_in, cross_down, cross_up, cross_bias, top_weight, d_hidden):
    scale_factor = 1.0 / math.sqrt(BATCH)
    owners = owner.reshape(SHARDS, LOOK_DEV)
    rows_all = row_in.reshape(SHARDS, LOOK_DEV)
    grads_all = d_hidden.reshape(SHARDS, B_DEV, H)

    def device_step(carry, inputs):
        dense_sum, hot_sum, cold_sum = carry
        dest_list, row_list, bag_list, grad_hidden = inputs
        is_hot = dest_list < N_WIDE
        hot_index = jnp.where(is_hot, dest_list * ROWS_DEV + row_list, 0).astype(jnp.int32)
        cold_index = jnp.where(is_hot, 0, (dest_list - N_WIDE) * ROWS_DEV + row_list).astype(jnp.int32)
        values = jnp.where(is_hot[:, None], hot_table[hot_index], cold_table[cold_index])
        pooled = jax.ops.segment_sum(values.astype(jnp.float32), bag_list, num_segments=BAGS_DEV)
        base = pooled.reshape(B_DEV, D).astype(jnp.bfloat16)
        terms, d_base = dense_pass(base, grad_hidden, cross_down, cross_up, cross_bias, top_weight)
        per_look = d_base.reshape(BAGS_DEV, E)[bag_list].astype(jnp.float32)
        hot_target = jnp.where(is_hot, hot_index, HOT).astype(jnp.int32)
        cold_target = jnp.where(is_hot, COLD, cold_index).astype(jnp.int32)
        hot_sum = hot_sum.at[hot_target].add(per_look, mode='drop')
        cold_sum = cold_sum.at[cold_target].add(per_look, mode='drop')
        dense_sum = dense_sum + terms * scale_factor
        return ((dense_sum, hot_sum, cold_sum), None)
    start_carry = (jnp.zeros((D, 2 * R + H), jnp.float32), jnp.zeros((HOT, E), jnp.float32), jnp.zeros((COLD, E), jnp.float32))
    final_carry, unused = lax.scan(device_step, start_carry, (owners, rows_all, bag_of, grads_all))
    dense_sum, hot_sum, cold_sum = final_carry
    return (dense_sum[:, :R], dense_sum[:, R:2 * R], dense_sum[:, 2 * R:], hot_sum, cold_sum)
```

```python
import functools
import math

import jax
import jax.numpy as jnp
from jax import lax
from jax.experimental import pallas as pl
from jax.experimental.pallas import tpu as pltpu
from jax.sharding import PartitionSpec as P

BF = jnp.bfloat16
F32 = jnp.float32
CAP = 64
LANES = 128


def nt_dot(a, b):
    return lax.dot_general(a, b, (((1,), (1,)), ((), ())), preferred_element_type=F32)


def tn_dot(a, b):
    return lax.dot_general(a, b, (((0,), (0,)), ((), ())), preferred_element_type=F32)


def onehot(mask):
    return jnp.where(mask, 1.0, 0.0).astype(BF)


def index_kernel(dest_ref, row_ref, bag_ref, req_ref, bagp_ref, acc_ref, run_ref):
    blocks, width = dest_ref.shape
    dests = run_ref.shape[0]
    slot_rows = req_ref.shape[0]
    upper = lax.broadcasted_iota(jnp.int32, (width, width), 0) < lax.broadcasted_iota(
        jnp.int32, (width, width), 1
    )
    tri = jnp.concatenate([onehot(upper), jnp.ones((width, LANES), BF)], axis=1)
    dest_iota = lax.broadcasted_iota(jnp.int32, (dests, width), 0)
    row_iota = lax.broadcasted_iota(jnp.int32, (slot_rows, width), 0)
    lane_iota = lax.broadcasted_iota(jnp.int32, (LANES, width), 0)
    run_ref[...] = jnp.zeros_like(run_ref)
    acc_ref[...] = jnp.zeros_like(acc_ref)

    def step(k, carry):
        dest = dest_ref[pl.ds(k, 1), :]
        named = dest_iota == dest
        counts = jnp.dot(onehot(named), tri, preferred_element_type=F32)
        run = run_ref[...]
        earlier = counts[:, :width] + jnp.concatenate([run] * (width // LANES), axis=1)
        run_ref[...] = run + counts[:, width:]
        rank = jnp.sum(jnp.where(named, earlier, 0.0), axis=0, keepdims=True).astype(jnp.int32)
        slot = dest * CAP + rank
        left = onehot(row_iota == (slot >> 7))
        place = lane_iota == (slot & 127)
        row = row_ref[pl.ds(k, 1), :]
        bag = bag_ref[pl.ds(k, 1), :]
        parts = []
        for value in ((row >> 7) + 1, row & 127, (bag >> 7) + 1, bag & 127):
            parts.append(jnp.where(place, value.astype(F32), 0.0).astype(BF))
        acc_ref[...] += nt_dot(left, jnp.concatenate(parts, axis=0))
        return carry

    lax.fori_loop(0, blocks, step, 0)
    acc = acc_ref[...].astype(jnp.int32)
    req_ref[...] = (acc[:, :LANES] - 1) * 128 + acc[:, LANES : 2 * LANES]
    bag = (acc[:, 2 * LANES : 3 * LANES] - 1) * 128 + acc[:, 3 * LANES :]
    bagp_ref[...] = jnp.where(bag < 0, -128, (bag & 31) * 128 + (bag >> 5))


def columns_of(idx_row):
    return jnp.transpose(jnp.broadcast_to(idx_row, (LANES, LANES)))


def gather_rows(idx_row, weights, low):
    groups = weights.shape[1] // LANES
    index = columns_of(idx_row)
    lo, hi = index & (low - 1), index >> (low.bit_length() - 1)
    lane = lax.broadcasted_iota(jnp.int32, (LANES, LANES), 1)
    pick = jnp.concatenate([onehot(lo == lane + LANES * t) for t in range(low // LANES)], axis=1)
    found = jnp.dot(pick, weights, preferred_element_type=F32)
    rows = found[:, :LANES]
    for h in range(1, groups):
        rows = jnp.where(hi == h, found[:, h * LANES : (h + 1) * LANES], rows)
    return rows.astype(BF)


def add_rows(idx, rows_ref, start, count, low, groups):
    tall = lax.broadcasted_iota(jnp.int32, (low, LANES), 0)
    lefts, rights = [], []
    for t in range(count // LANES):
        idx_row = idx[t : t + 1, :]
        lefts.append(onehot(tall == (idx_row & (low - 1))))
        hi = columns_of(idx_row) >> (low.bit_length() - 1)
        rows = rows_ref[pl.ds(start + t * LANES, LANES), :]
        rights.append(
            jnp.concatenate(
                [jnp.where(hi == h, rows, jnp.zeros((), BF)) for h in range(groups)], axis=1
            )
        )
    return jnp.dot(
        jnp.concatenate(lefts, axis=1), jnp.concatenate(rights, axis=0), preferred_element_type=F32
    )


def fold(table_ref, folded_ref):
    low = folded_ref.shape[0]
    for h in range(folded_ref.shape[1] // LANES):
        folded_ref[:, h * LANES : (h + 1) * LANES] = table_ref[h * low : (h + 1) * low, :]


def holder_kernel(idx_ref, table_ref, out_ref, folded_ref):
    fold(table_ref, folded_ref)

    def step(k, carry):
        out_ref[pl.ds(pl.multiple_of(k * LANES, LANES), LANES), :] = gather_rows(
            idx_ref[pl.ds(k, 1), :], folded_ref[...], folded_ref.shape[0]
        )
        return carry

    lax.fori_loop(0, idx_ref.shape[0], step, 0)


def accumulate_kernel(idx_ref, rows_ref, out_ref, acc_ref):
    low = acc_ref.shape[0]
    groups = acc_ref.shape[1] // LANES
    acc_ref[...] = jnp.zeros_like(acc_ref)
    per = 8

    def step(k, carry):
        idx = idx_ref[pl.ds(pl.multiple_of(k * per, per), per), :]
        acc_ref[...] += add_rows(
            idx, rows_ref, pl.multiple_of(k * per * LANES, LANES), per * LANES, low, groups
        )
        return carry

    lax.fori_loop(0, idx_ref.shape[0] // per, step, 0)
    for h in range(groups):
        out_ref[h * low : (h + 1) * low, :] = acc_ref[:, h * LANES : (h + 1) * LANES]


def pool_into(bagp_ref, rows_ref, first, acc_ref):
    per = 8
    low, groups = acc_ref.shape[0], acc_ref.shape[1] // LANES

    def step(k, carry):
        idx = bagp_ref[pl.ds(pl.multiple_of(first + k * per, per), per), :]
        acc_ref[...] += add_rows(
            idx, rows_ref, pl.multiple_of(k * per * LANES, LANES), per * LANES, low, groups
        )
        return carry

    lax.fori_loop(0, rows_ref.shape[0] // (per * LANES), step, 0)


def middle_kernel(
    batch,
    bagp_ref,
    hot_ref,
    cold_ref,
    down_hbm,
    up_hbm,
    bias_ref,
    top_hbm,
    dh_ref,
    out_hot_ref,
    out_cold_ref,
    grads_ref,
    down,
    up,
    top,
    acc_ref,
    base,
    cross,
    mixed,
    d_mixed,
    d_cross,
    d_base,
    sems,
):
    loads = [
        pltpu.make_async_copy(source, target, sems.at[n])
        for n, (source, target) in enumerate(((down_hbm, down), (up_hbm, up), (top_hbm, top)))
    ]
    for load in loads:
        load.start()
    acc_ref[...] = jnp.zeros_like(acc_ref)
    pool_into(bagp_ref, hot_ref, 0, acc_ref)
    pool_into(bagp_ref, cold_ref, hot_ref.shape[0] // LANES, acc_ref)
    for load in loads:
        load.wait()
    low_bags, groups = acc_ref.shape[0], acc_ref.shape[1] // LANES
    samples = base.shape[0]
    each = low_bags // samples
    features = each * groups
    for f in range(features):
        base[:, f * LANES : (f + 1) * LANES] = acc_ref[
            (f % each) * samples : (f % each + 1) * samples,
            (f // each) * LANES : (f // each + 1) * LANES,
        ].astype(BF)
    total = base.shape[1]
    step = 512
    spans = [slice(s, s + step) for s in range(0, total, step)]
    low = jnp.dot(base[...], down[...], preferred_element_type=F32).astype(BF)
    preact = jnp.zeros(dh_ref.shape, F32)
    for span in spans:
        part = nt_dot(low, up[span, :]) + bias_ref[:, span]
        full = base[:, span].astype(F32)
        joined = (full * part + full).astype(BF)
        cross[:, span] = part
        mixed[:, span] = joined
        preact += jnp.dot(joined, top[span, :], preferred_element_type=F32)
    sg = 1.0 / (1.0 + jnp.exp(-preact))
    d_pre = (dh_ref[...].astype(F32) * sg * (1.0 + preact * (1.0 - sg))).astype(BF)
    d_low_sum = jnp.zeros(low.shape, F32)
    for span in spans:
        part = nt_dot(d_pre, top[span, :])
        d_mixed[:, span] = part
        crossed = (part * base[:, span].astype(F32)).astype(BF)
        d_cross[:, span] = crossed
        d_low_sum += jnp.dot(crossed, up[span, :], preferred_element_type=F32)
    d_low = d_low_sum.astype(BF)
    for n, span in enumerate(spans):
        part = (d_mixed[:, span] * (cross[:, span] + 1.0) + nt_dot(d_low, down[span, :])).astype(BF)
        for g in range(step // LANES):
            f = n * (step // LANES) + g
            d_base[
                (f % each) * samples : (f % each + 1) * samples,
                (f // each) * LANES : (f // each + 1) * LANES,
            ] = part[:, g * LANES : (g + 1) * LANES]
    scale = 1.0 / math.sqrt(batch)
    rank = low.shape[1]
    for span in spans:
        grads_ref[span, :rank] = (tn_dot(d_cross[:, span], low) * scale).astype(grads_ref.dtype)
        grads_ref[span, rank : 2 * rank] = (tn_dot(base[:, span], d_low) * scale).astype(
            grads_ref.dtype
        )
        grads_ref[span, 2 * rank :] = (tn_dot(mixed[:, span], d_pre) * scale).astype(
            grads_ref.dtype
        )
    hot_rows = out_hot_ref.shape[0] // LANES

    def send_block(out, first):
        def body(k, carry):
            out[pl.ds(pl.multiple_of(k * LANES, LANES), LANES), :] = gather_rows(
                bagp_ref[pl.ds(first + k, 1), :], d_base[...], low_bags
            )
            return carry

        lax.fori_loop(0, out.shape[0] // LANES, body, 0)

    send_block(out_hot_ref, 0)
    send_block(out_cold_ref, hot_rows)


VM = pl.BlockSpec(memory_space=pltpu.VMEM)
ANY = pl.BlockSpec(memory_space=pl.ANY)
LIMIT = 56 << 20


def params(**more):
    return pltpu.CompilerParams(vmem_limit_bytes=LIMIT, **more)


def index_call(dest, row, bag, dests):
    looks = dest.shape[0]
    slot_rows = dests * CAP // LANES
    shape = (looks // 256, 256)
    return pl.pallas_call(
        index_kernel,
        out_shape=[jax.ShapeDtypeStruct((slot_rows, LANES), jnp.int32)] * 2,
        in_specs=[VM] * 3,
        out_specs=[VM] * 2,
        scratch_shapes=[pltpu.VMEM((slot_rows, 4 * LANES), F32), pltpu.VMEM((dests, LANES), F32)],
        compiler_params=params(),
        name="index",
    )(dest.reshape(shape), row.reshape(shape), bag.reshape(shape))


def holder_call(idx, table):
    return pl.pallas_call(
        holder_kernel,
        out_shape=jax.ShapeDtypeStruct((idx.size, LANES), BF),
        in_specs=[VM] * 2,
        out_specs=VM,
        scratch_shapes=[pltpu.VMEM((512, table.shape[0] // 512 * LANES), BF)],
        compiler_params=params(),
        name="holder",
    )(idx, table)


def accumulate_call(idx, rows, table_rows):
    return pl.pallas_call(
        accumulate_kernel,
        out_shape=jax.ShapeDtypeStruct((table_rows, LANES), F32),
        in_specs=[VM] * 2,
        out_specs=VM,
        scratch_shapes=[pltpu.VMEM((512, table_rows // 512 * LANES), F32)],
        compiler_params=params(),
        name="accumulate",
    )(idx, rows)


def middle_call(bagp, hot, cold, down, up, bias, top, d_hidden, batch, grads_dtype):
    samples = d_hidden.shape[0]
    total, rank = down.shape
    units = top.shape[1]
    low_bags = 1024
    groups = total // LANES * samples // low_bags
    return pl.pallas_call(
        functools.partial(middle_kernel, batch),
        out_shape=[
            jax.ShapeDtypeStruct(hot.shape, BF),
            jax.ShapeDtypeStruct(cold.shape, BF),
            jax.ShapeDtypeStruct((total, 2 * rank + units), grads_dtype),
        ],
        in_specs=[VM, VM, VM, ANY, ANY, VM, ANY, VM],
        out_specs=[VM] * 3,
        scratch_shapes=[
            pltpu.VMEM((total, rank), BF),
            pltpu.VMEM((total, rank), BF),
            pltpu.VMEM((total, units), BF),
            pltpu.VMEM((low_bags, groups * LANES), F32),
            pltpu.VMEM((samples, total), BF),
            pltpu.VMEM((samples, total), F32),
            pltpu.VMEM((samples, total), BF),
            pltpu.VMEM((samples, total), F32),
            pltpu.VMEM((samples, total), BF),
            pltpu.VMEM((low_bags, groups * LANES), BF),
            pltpu.SemaphoreType.DMA((3,)),
        ],
        compiler_params=params(),
        name="middle",
    )(bagp, hot, cold, down, up, bias.reshape(1, total), top, d_hidden)


def exchange(value, axes):
    return lax.all_to_all(value, axes, split_axis=0, concat_axis=0, tiled=True)


def body(
    hot_table,
    cold_table,
    bag_of,
    owner,
    row_in,
    cross_down,
    cross_up,
    cross_bias,
    top_weight,
    d_hidden,
):
    n_rep = lax.axis_size("rep")
    n_wide = lax.axis_size("wide")
    shards = n_rep * n_wide
    both = ("rep", "wide")
    rows_dev, width = hot_table.shape
    feat_width, rank = cross_down.shape
    batch = d_hidden.shape[0] * shards
    req, bagp = index_call(owner[:, 0], row_in, bag_of[0], n_wide + shards)
    hot_lanes = n_wide * CAP // LANES
    hot_asked = exchange(req[:hot_lanes].reshape(n_wide, CAP), "wide").reshape(-1, LANES)
    cold_asked = exchange(req[hot_lanes:].reshape(shards, CAP), both).reshape(-1, LANES)
    cold_rows = exchange(holder_call(cold_asked, cold_table).reshape(shards, CAP, width), both)
    hot_rows = exchange(holder_call(hot_asked, hot_table).reshape(n_wide, CAP, width), "wide")
    out_hot, out_cold, terms = middle_call(
        bagp,
        hot_rows.reshape(-1, width),
        cold_rows.reshape(-1, width),
        cross_down,
        cross_up,
        cross_bias,
        top_weight,
        d_hidden,
        batch,
        F32,
    )
    share = feat_width // shards
    partial = lax.psum_scatter(
        terms.reshape(n_rep, n_wide, share, -1), "wide", scatter_dimension=1, tiled=True
    )
    summed = exchange(partial.reshape(n_rep, share, -1), "rep").sum(axis=0)
    cold_in = exchange(out_cold.reshape(shards, CAP, width), both).reshape(-1, width)
    hot_in = exchange(out_hot.reshape(n_wide, CAP, width), "wide").reshape(-1, width)
    hot_part = accumulate_call(hot_asked, hot_in, rows_dev)
    pieces = exchange(hot_part.reshape(n_rep, rows_dev // n_rep, width), "rep").sum(axis=0)
    hot_grad = lax.all_gather(pieces, "rep", tiled=True)
    cold_grad = accumulate_call(cold_asked, cold_in, rows_dev)
    return (
        summed[:, :rank],
        summed[:, rank : 2 * rank],
        summed[:, 2 * rank :],
        hot_grad,
        cold_grad,
    )


def solution(mesh):
    placed = (
        P("wide", None),
        P(("rep", "wide"), None),
        P(("rep", "wide"), None),
        P(("rep", "wide"), None),
        P(("rep", "wide")),
        P(),
        P(),
        P(),
        P(),
        P(("rep", "wide"), None),
    )
    return jax.shard_map(
        body,
        mesh=mesh,
        in_specs=placed,
        out_specs=(
            P(("rep", "wide"), None),
            P(("rep", "wide"), None),
            P(("rep", "wide"), None),
            P("wide", None),
            P(("rep", "wide"), None),
        ),
        check_vma=False,
    )
```

```python
import functools
import math

import jax
import jax.numpy as jnp
from jax import lax
from jax.experimental import pallas as pl
from jax.experimental.pallas import tpu as pltpu
from jax.sharding import PartitionSpec as P

BF = jnp.bfloat16
F32 = jnp.float32
CAP = 64
LANES = 128


def nt_dot(a, b):
    return lax.dot_general(a, b, (((1,), (1,)), ((), ())), preferred_element_type=F32)


def tn_dot(a, b):
    return lax.dot_general(a, b, (((0,), (0,)), ((), ())), preferred_element_type=F32)


def onehot(mask):
    return jnp.where(mask, 1.0, 0.0).astype(BF)


def index_kernel(dest_ref, row_ref, bag_ref, ask_ref, bagp_ref, acc_ref, run_ref):
    blocks, width = dest_ref.shape
    dests = run_ref.shape[0]
    slot_rows = bagp_ref.shape[0]
    upper = lax.broadcasted_iota(jnp.int32, (width, width), 0) < lax.broadcasted_iota(
        jnp.int32, (width, width), 1
    )
    tri = jnp.concatenate([onehot(upper), jnp.ones((width, LANES), BF)], axis=1)
    dest_iota = lax.broadcasted_iota(jnp.int32, (dests, width), 0)
    row_iota = lax.broadcasted_iota(jnp.int32, (slot_rows, width), 0)
    lane_iota = lax.broadcasted_iota(jnp.int32, (LANES, width), 0)
    run_ref[...] = jnp.zeros_like(run_ref)
    acc_ref[...] = jnp.zeros_like(acc_ref)

    per = 4

    def step(k, carry):
        run = run_ref[...]
        total = acc_ref[...]
        for t in range(per):
            at = pl.ds(k * per + t, 1)
            dest = dest_ref[at, :]
            named = dest_iota == dest
            counts = jnp.dot(onehot(named), tri, preferred_element_type=F32)
            earlier = counts[:, :width] + jnp.concatenate([run] * (width // LANES), axis=1)
            run = run + counts[:, width:]
            rank = jnp.sum(jnp.where(named, earlier, 0.0), axis=0, keepdims=True).astype(jnp.int32)
            slot = dest * CAP + rank
            left = onehot(row_iota == (slot >> 7))
            place = lane_iota == (slot & 127)
            row = row_ref[at, :]
            bag = bag_ref[at, :]
            parts = []
            for value in ((row >> 7) + 1, row & 127, (bag >> 7) + 1, bag & 127):
                parts.append(jnp.where(place, value.astype(F32), 0.0).astype(BF))
            total = total + nt_dot(left, jnp.concatenate(parts, axis=0))
        run_ref[...] = run
        acc_ref[...] = total
        return carry

    lax.fori_loop(0, blocks // per, step, 0)
    acc = acc_ref[...].astype(jnp.int32)
    req = (acc[:, :LANES] - 1) * 128 + acc[:, LANES : 2 * LANES]
    half = ask_ref.shape[0] // 2
    cold = req[slot_rows - half :, :]
    hot = jnp.concatenate([req[: slot_rows - half, :]] * (half // (slot_rows - half)), axis=0)
    first = lax.broadcasted_iota(jnp.int32, cold.shape, 1) < CAP
    ask_ref[pl.ds(0, half, stride=2), :] = jnp.where(first, cold, pltpu.roll(hot, CAP, 1))
    ask_ref[pl.ds(1, half, stride=2), :] = jnp.where(first, pltpu.roll(cold, CAP, 1), hot)
    bag = (acc[:, 2 * LANES : 3 * LANES] - 1) * 128 + acc[:, 3 * LANES :]
    bagp_ref[...] = jnp.where(bag < 0, -128, (bag & 31) * 128 + (bag >> 5))


def columns_of(idx_row):
    return jnp.transpose(jnp.broadcast_to(idx_row, (LANES, LANES)))


def gather_rows(idx, weights, low):
    groups = weights.shape[1] // LANES
    shift = low.bit_length() - 1
    lane = lax.broadcasted_iota(jnp.int32, (LANES, LANES), 1)
    picks, his = [], []
    for t in range(idx.shape[0]):
        index = columns_of(idx[t : t + 1, :])
        lo = index & (low - 1)
        his.append(index >> shift)
        picks.append(
            jnp.concatenate([onehot(lo == lane + LANES * u) for u in range(low // LANES)], axis=1)
        )
    found = jnp.dot(jnp.concatenate(picks, axis=0), weights, preferred_element_type=F32)
    hi = jnp.concatenate(his, axis=0)
    rows = found[:, :LANES]
    for h in range(1, groups):
        rows = jnp.where(hi == h, found[:, h * LANES : (h + 1) * LANES], rows)
    return rows.astype(BF)


def gather_all(idx_ref, first, weights_ref, out_ref, per):
    size = per * LANES

    def step(k, carry):
        idx = idx_ref[pl.ds(pl.multiple_of(first + k * per, per), per), :]
        out_ref[pl.ds(pl.multiple_of(k * size, size), size), :] = gather_rows(
            idx, weights_ref[...], weights_ref.shape[0]
        )
        return carry

    lax.fori_loop(0, out_ref.shape[0] // size, step, 0)


def add_rows(idx, rows_ref, start, count, low, groups):
    tall = lax.broadcasted_iota(jnp.int32, (low, LANES), 0)
    lefts, rights = [], []
    for t in range(count // LANES):
        idx_row = idx[t : t + 1, :]
        lefts.append(onehot(tall == (idx_row & (low - 1))))
        hi = columns_of(idx_row) >> (low.bit_length() - 1)
        rows = rows_ref[pl.ds(start + t * LANES, LANES), :]
        rights.append(
            jnp.concatenate(
                [jnp.where(hi == h, rows, jnp.zeros((), BF)) for h in range(groups)], axis=1
            )
        )
    return jnp.dot(
        jnp.concatenate(lefts, axis=1), jnp.concatenate(rights, axis=0), preferred_element_type=F32
    )


def fold(table_ref, folded_ref):
    low = folded_ref.shape[0]
    for h in range(folded_ref.shape[1] // LANES):
        folded_ref[:, h * LANES : (h + 1) * LANES] = table_ref[h * low : (h + 1) * low, :]


def holder_kernel(
    n_wide, asked_ref, hot_ref, cold_ref, hot_rows, cold_rows, hot_idx, cold_idx, fold_hot, fold_cold
):
    fold(hot_ref, fold_hot)
    fold(cold_ref, fold_cold)
    half = asked_ref.shape[0] // 2
    count = n_wide // 2
    begin = lax.axis_index("rep") * n_wide
    even, odd = asked_ref[pl.ds(0, half, stride=2), :], asked_ref[pl.ds(1, half, stride=2), :]
    first = lax.broadcasted_iota(jnp.int32, even.shape, 1) < CAP
    cold_idx[...] = jnp.where(first, even, pltpu.roll(odd, CAP, 1))
    even = asked_ref[pl.ds(begin, count, stride=2), :]
    odd = asked_ref[pl.ds(begin + 1, count, stride=2), :]
    hot_idx[...] = jnp.where(first[:count], pltpu.roll(even, CAP, 1), odd)
    gather_all(cold_idx, 0, fold_cold, cold_rows, 8)
    gather_all(hot_idx, 0, fold_hot, hot_rows, 8)


def accumulate_kernel(idx_ref, rows_ref, out_ref, acc_ref):
    low = acc_ref.shape[0]
    groups = acc_ref.shape[1] // LANES
    acc_ref[...] = jnp.zeros_like(acc_ref)
    per = 8

    def step(k, carry):
        idx = idx_ref[pl.ds(pl.multiple_of(k * per, per), per), :]
        acc_ref[...] += add_rows(
            idx, rows_ref, pl.multiple_of(k * per * LANES, LANES), per * LANES, low, groups
        )
        return carry

    lax.fori_loop(0, idx_ref.shape[0] // per, step, 0)
    for h in range(groups):
        out_ref[h * low : (h + 1) * low, :] = acc_ref[:, h * LANES : (h + 1) * LANES]


def pool_into(bagp_ref, rows_ref, first, acc_ref):
    per = 8
    low, groups = acc_ref.shape[0], acc_ref.shape[1] // LANES

    def step(k, carry):
        idx = bagp_ref[pl.ds(pl.multiple_of(first + k * per, per), per), :]
        acc_ref[...] += add_rows(
            idx, rows_ref, pl.multiple_of(k * per * LANES, LANES), per * LANES, low, groups
        )
        return carry

    lax.fori_loop(0, rows_ref.shape[0] // (per * LANES), step, 0)


def pool_kernel(bagp_ref, hot_ref, cold_ref, base_ref, acc_ref):
    acc_ref[...] = jnp.zeros_like(acc_ref)
    pool_into(bagp_ref, hot_ref, 0, acc_ref)
    pool_into(bagp_ref, cold_ref, hot_ref.shape[0] // LANES, acc_ref)
    samples = base_ref.shape[0]
    each = acc_ref.shape[0] // samples
    for f in range(base_ref.shape[1] // LANES):
        base_ref[:, f * LANES : (f + 1) * LANES] = acc_ref[
            (f % each) * samples : (f % each + 1) * samples,
            (f // each) * LANES : (f // each + 1) * LANES,
        ].astype(BF)


def dense_kernel(
    batch,
    base,
    down,
    up,
    bias_ref,
    top,
    dh_ref,
    d_base,
    grads_ref,
    cross,
    mixed,
    d_mixed,
    d_cross,
):
    samples, total = base.shape
    each = d_base.shape[0] // samples
    step = 512
    spans = [slice(s, s + step) for s in range(0, total, step)]
    low = jnp.dot(base[...], down[...], preferred_element_type=F32).astype(BF)
    preact = jnp.zeros(dh_ref.shape, F32)
    for span in spans:
        part = nt_dot(low, up[span, :]) + bias_ref[:, span]
        full = base[:, span].astype(F32)
        joined = (full * part + full).astype(BF)
        cross[:, span] = part
        mixed[:, span] = joined
        preact += jnp.dot(joined, top[span, :], preferred_element_type=F32)
    sg = 1.0 / (1.0 + jnp.exp(-preact))
    d_pre = (dh_ref[...].astype(F32) * sg * (1.0 + preact * (1.0 - sg))).astype(BF)
    d_low_sum = jnp.zeros(low.shape, F32)
    for span in spans:
        part = nt_dot(d_pre, top[span, :])
        d_mixed[:, span] = part
        crossed = (part * base[:, span].astype(F32)).astype(BF)
        d_cross[:, span] = crossed
        d_low_sum += jnp.dot(crossed, up[span, :], preferred_element_type=F32)
    d_low = d_low_sum.astype(BF)
    for n, span in enumerate(spans):
        part = (d_mixed[:, span] * (cross[:, span] + 1.0) + nt_dot(d_low, down[span, :])).astype(BF)
        for g in range(step // LANES):
            f = n * (step // LANES) + g
            d_base[
                (f % each) * samples : (f % each + 1) * samples,
                (f // each) * LANES : (f // each + 1) * LANES,
            ] = part[:, g * LANES : (g + 1) * LANES]
    scale = 1.0 / math.sqrt(batch)
    rank = low.shape[1]
    for span in spans:
        grads_ref[span, :rank] = (tn_dot(d_cross[:, span], low) * scale).astype(grads_ref.dtype)
        grads_ref[span, rank : 2 * rank] = (tn_dot(base[:, span], d_low) * scale).astype(
            grads_ref.dtype
        )
        grads_ref[span, 2 * rank :] = (tn_dot(mixed[:, span], d_pre) * scale).astype(
            grads_ref.dtype
        )


def send_kernel(bagp_ref, d_base_ref, hot_ref, cold_ref):
    gather_all(bagp_ref, 0, d_base_ref, hot_ref, 4)
    gather_all(bagp_ref, hot_ref.shape[0] // LANES, d_base_ref, cold_ref, 4)


VM = pl.BlockSpec(memory_space=pltpu.VMEM)
ANY = pl.BlockSpec(memory_space=pl.ANY)
LIMIT = 56 << 20


def params(**more):
    return pltpu.CompilerParams(vmem_limit_bytes=LIMIT, **more)


def index_call(dest, row, bag, n_wide, shards):
    looks = dest.shape[0]
    dests = n_wide + shards
    slot_rows = dests * CAP // LANES
    shape = (looks // 256, 256)
    return pl.pallas_call(
        index_kernel,
        out_shape=[
            jax.ShapeDtypeStruct((shards, LANES), jnp.int32),
            jax.ShapeDtypeStruct((slot_rows, LANES), jnp.int32),
        ],
        in_specs=[VM] * 3,
        out_specs=[VM] * 2,
        scratch_shapes=[pltpu.VMEM((slot_rows, 4 * LANES), F32), pltpu.VMEM((dests, LANES), F32)],
        compiler_params=params(),
        name="index",
    )(dest.reshape(shape), row.reshape(shape), bag.reshape(shape))


def holder_call(asked, hot_table, cold_table, n_wide):
    shards = asked.shape[0]
    slots = (n_wide * CAP, shards * CAP)
    return pl.pallas_call(
        functools.partial(holder_kernel, n_wide),
        out_shape=[jax.ShapeDtypeStruct((s, LANES), BF) for s in slots]
        + [jax.ShapeDtypeStruct((s // LANES, LANES), jnp.int32) for s in slots],
        in_specs=[VM] * 3,
        out_specs=[VM] * 4,
        scratch_shapes=[
            pltpu.VMEM((512, table.shape[0] // 512 * LANES), BF) for table in (hot_table, cold_table)
        ],
        compiler_params=params(),
        name="holder",
    )(asked, hot_table, cold_table)


def accumulate_call(idx, rows, table_rows):
    return pl.pallas_call(
        accumulate_kernel,
        out_shape=jax.ShapeDtypeStruct((table_rows, LANES), F32),
        in_specs=[VM] * 2,
        out_specs=VM,
        scratch_shapes=[pltpu.VMEM((512, table_rows // 512 * LANES), F32)],
        compiler_params=params(),
        name="accumulate",
    )(idx, rows)


def pool_call(bagp, hot, cold, samples):
    low_bags = 1024
    bags_groups = 4
    total = low_bags * bags_groups // samples * LANES
    return pl.pallas_call(
        pool_kernel,
        out_shape=jax.ShapeDtypeStruct((samples, total), BF),
        in_specs=[VM] * 3,
        out_specs=VM,
        scratch_shapes=[pltpu.VMEM((low_bags, bags_groups * LANES), F32)],
        compiler_params=params(),
        name="pool",
    )(bagp, hot, cold)


def dense_call(base, down, up, bias, top, d_hidden, batch, grads_dtype):
    samples, total = base.shape
    rank, units = down.shape[1], top.shape[1]
    low_bags = 1024
    groups = total // LANES * samples // low_bags
    return pl.pallas_call(
        functools.partial(dense_kernel, batch),
        out_shape=[
            jax.ShapeDtypeStruct((low_bags, groups * LANES), BF),
            jax.ShapeDtypeStruct((total, 2 * rank + units), grads_dtype),
        ],
        in_specs=[VM] * 6,
        out_specs=[VM] * 2,
        scratch_shapes=[
            pltpu.VMEM((samples, total), F32),
            pltpu.VMEM((samples, total), BF),
            pltpu.VMEM((samples, total), F32),
            pltpu.VMEM((samples, total), BF),
        ],
        compiler_params=params(),
        name="dense",
    )(base, down, up, bias.reshape(1, total), top, d_hidden)


def send_call(bagp, d_base, hot_slots):
    return pl.pallas_call(
        send_kernel,
        out_shape=[
            jax.ShapeDtypeStruct((hot_slots, LANES), BF),
            jax.ShapeDtypeStruct((bagp.size - hot_slots, LANES), BF),
        ],
        in_specs=[VM] * 2,
        out_specs=[VM] * 2,
        compiler_params=params(),
        name="send",
    )(bagp, d_base)


MESH = pl.DeviceIdType.MESH


def place():
    y, wide = lax.axis_index("rep"), lax.axis_index("wide")
    return y, wide // 8, (wide // 2) % 4, wide % 2


def sum_kernel(streams, t_ref, out_ref, core_in, first, in1, second, in2, third, in3, sends, recvs):
    y, x, z, c = place()
    here = (y, x, z)
    barrier = pltpu.get_barrier_semaphore()

    def device(pos, core):
        return (pos[0], pos[1] * 8 + pos[2] * 2 + core)

    def moved(axis, by):
        return tuple((p + by) % 4 if n == axis else p for n, p in enumerate(here))

    partners = [device(here, 1 - c)]
    partners += [device(moved(axis, by), c) for axis in range(3) for by in (1, 2, 3)]
    for partner in partners:
        pl.semaphore_signal(barrier, inc=1, device_id=partner, device_id_type=MESH)
    pl.semaphore_wait(barrier, len(partners))

    def send(n, source, target, partner):
        copy = pltpu.make_async_remote_copy(
            src_ref=source,
            dst_ref=target,
            send_sem=sends.at[n],
            recv_sem=recvs.at[n],
            device_id=partner,
            device_id_type=MESH,
        )
        copy.start()
        return copy

    started = []
    waiting = []
    for n, (cols, order) in enumerate(streams):
        waiting.append(
            send(n, t_ref.at[:, :, :, 1 - c, :, cols], core_in.at[:, :, :, :, cols], device(here, 1 - c))
        )
    started += waiting
    number = len(streams)

    def fan(source, target, cols, axis, rank):
        nonlocal number
        copies = []
        for by in (2, 1, 3):
            to = moved(axis, by)
            index = tuple(to[axis] if d == rank else slice(None) for d in range(rank + 1))
            copies.append(
                send(number, source.at[(*index, Ellipsis, cols)], target.at[by - 1, ..., cols], device(to, c))
            )
            number += 1
        return copies

    rests = [[a for a in range(3)] for _ in streams]
    stage = []
    for n, (cols, order) in enumerate(streams):
        waiting[n].wait_recv()

        def add(i, carry):
            at = (i // 16, (i // 4) % 4, i % 4)
            own = t_ref[(*at, c, slice(None), cols)].astype(F32)
            first[(*at, slice(None), cols)] = (
                own + core_in[(*at, slice(None), cols)].astype(F32)
            ).astype(BF)
            return carry

        lax.fori_loop(0, 64, add, 0)
        rank = rests[n].index(order[0])
        stage.append(fan(first, in1, cols, order[0], rank))
    started += sum(stage, [])
    after = []
    for n, (cols, order) in enumerate(streams):
        for copy in stage[n]:
            copy.wait_recv()
        rank = rests[n].index(order[0])

        def add(i, carry):
            at = [i // 4, i % 4]
            own = list(at)
            own.insert(rank, here[order[0]])
            total = first[(*own, slice(None), cols)].astype(F32)
            for k in range(3):
                total += in1[(k, *at, slice(None), cols)].astype(F32)
            second[(*at, slice(None), cols)] = total.astype(BF)
            return carry

        lax.fori_loop(0, 16, add, 0)
        rests[n].remove(order[0])
        after.append(fan(second, in2, cols, order[1], rests[n].index(order[1])))
    started += sum(after, [])
    last = []
    for n, (cols, order) in enumerate(streams):
        for copy in after[n]:
            copy.wait_recv()
        rank = rests[n].index(order[1])

        def add(i, carry):
            own = [i]
            own.insert(rank, here[order[1]])
            total = second[(*own, slice(None), cols)].astype(F32)
            for k in range(3):
                total += in2[(k, i, slice(None), cols)].astype(F32)
            third[i, :, cols] = total
            return carry

        lax.fori_loop(0, 4, add, 0)
        rests[n].remove(order[1])
        last.append(fan(third, in3, cols, order[2], 0))
    started += sum(last, [])
    for n, (cols, order) in enumerate(streams):
        for copy in last[n]:
            copy.wait_recv()
        total = third[here[order[2]], :, cols]
        for k in range(3):
            total += in3[k, :, cols]
        out_ref[:, cols] = total
    for copy in started:
        copy.wait_send()


def sum_call(terms, share):
    columns = terms.shape[1]
    step = columns // 8 // LANES * LANES
    cuts = [0, 3 * step, 6 * step, columns]
    orders = ((0, 1, 2), (1, 2, 0), (2, 0, 1))
    streams = [(slice(cuts[n], cuts[n + 1]), orders[n]) for n in range(3)]
    copies = 3 + 27
    return pl.pallas_call(
        functools.partial(sum_kernel, streams),
        out_shape=jax.ShapeDtypeStruct((share, columns), F32),
        in_specs=[VM],
        out_specs=VM,
        scratch_shapes=[
            pltpu.VMEM((4, 4, 4, share, columns), BF),
            pltpu.VMEM((4, 4, 4, share, columns), BF),
            pltpu.VMEM((3, 4, 4, share, columns), BF),
            pltpu.VMEM((4, 4, share, columns), BF),
            pltpu.VMEM((3, 4, share, columns), BF),
            pltpu.VMEM((4, share, columns), F32),
            pltpu.VMEM((3, share, columns), F32),
            pltpu.SemaphoreType.DMA((copies,)),
            pltpu.SemaphoreType.DMA((copies,)),
        ],
        compiler_params=params(collective_id=1, has_side_effects=True),
        name="dense_sum",
    )(terms.reshape(4, 4, 4, 2, share, columns))


def exchange(value, axes):
    return lax.all_to_all(value, axes, split_axis=0, concat_axis=0, tiled=True)


def body(
    hot_table,
    cold_table,
    bag_of,
    owner,
    row_in,
    cross_down,
    cross_up,
    cross_bias,
    top_weight,
    d_hidden,
):
    n_rep = lax.axis_size("rep")
    n_wide = lax.axis_size("wide")
    shards = n_rep * n_wide
    both = ("rep", "wide")
    rows_dev, width = hot_table.shape
    feat_width, rank = cross_down.shape
    batch = d_hidden.shape[0] * shards
    ask, bagp = index_call(owner[:, 0], row_in, bag_of[0], n_wide, shards)
    asked = exchange(ask[:, None, :], both).reshape(shards, LANES)
    hot_found, cold_found, hot_asked, cold_asked = holder_call(asked, hot_table, cold_table, n_wide)
    hot_rows = exchange(hot_found.reshape(n_wide, CAP, width), "wide").reshape(-1, width)
    cold_rows = exchange(cold_found.reshape(shards, CAP, width), both).reshape(-1, width)
    base = pool_call(bagp, hot_rows, cold_rows, d_hidden.shape[0])
    d_base, terms = dense_call(
        base, cross_down, cross_up, cross_bias, top_weight, d_hidden, batch, BF
    )
    out_hot, out_cold = send_call(bagp, d_base, n_wide * CAP)
    hot_in = exchange(out_hot.reshape(n_wide, CAP, width), "wide").reshape(-1, width)
    cold_in = exchange(out_cold.reshape(shards, CAP, width), both).reshape(-1, width)
    summed = sum_call(terms, feat_width // shards)
    hot_part = accumulate_call(hot_asked, hot_in, rows_dev)
    pieces = exchange(hot_part.reshape(n_rep, rows_dev // n_rep, width), "rep").sum(axis=0)
    hot_grad = lax.all_gather(pieces, "rep", tiled=True)
    cold_grad = accumulate_call(cold_asked, cold_in, rows_dev)
    return (
        summed[:, :rank],
        summed[:, rank : 2 * rank],
        summed[:, 2 * rank :],
        hot_grad,
        cold_grad,
    )


def solution(mesh):
    placed = (
        P("wide", None),
        P(("rep", "wide"), None),
        P(("rep", "wide"), None),
        P(("rep", "wide"), None),
        P(("rep", "wide")),
        P(),
        P(),
        P(),
        P(),
        P(("rep", "wide"), None),
    )
    return jax.shard_map(
        body,
        mesh=mesh,
        in_specs=placed,
        out_specs=(
            P(("rep", "wide"), None),
            P(("rep", "wide"), None),
            P(("rep", "wide"), None),
            P("wide", None),
            P(("rep", "wide"), None),
        ),
        check_vma=False,
    )
```
